256 devices in a mesh: energy: 8 (over y_hi, x), block: 32 (over y_lo, z, core).
Axes of the slice: x: 4, y: 4 (y_hi: 2, y_lo: 2; y = y_hi * 2 + y_lo), z: 8, core: 2. Of those that a mesh axis runs over, the one named last changes fastest.
Arguments:
- g_less: bfloat16 [256, 32, 128, 128], P('energy', 'block'), may hold values from -6 to 6
- g_great: bfloat16 [256, 32, 128, 128], P('energy', 'block'), may hold values from -6 to 6
- coupling: bfloat16 [32, 3, 128, 128], P('block'), may hold values from -0.3125 to 0.3125
- coupling_mask: int32 [32, 2], P('block'), may hold values 0 or 1
Outputs:
- sigma_less: float32 [256, 32, 128, 128], P('energy', 'block')
The draws below stay inside these ranges and needn't reach their ends.
All inputs are finite; a program needn't handle non-finite values. No bound on the sum of `coupling_mask` on one device may be relied on, other than what follows from the above.
Results may differ from the reference program's by a relative error of at most 0.009.
Values may be sent and summed in bfloat16 or wider, within the bound.
A program may use at most 64 MiB of HBM per device.

```python
import math
import jax
import jax.numpy as jnp
from jax import lax

ORB = 128
NE = 256
NB = 32


def plant(drawn, own_key, low, top_value):
    place = [jax.random.randint(jax.random.fold_in(own_key, axis), (), 0, length) for axis, length in enumerate(drawn.shape)]
    longest = drawn.shape.index(max(drawn.shape))
    beside = place[:longest] + [(place[longest] + 1) % drawn.shape[longest]] + place[longest + 1:]
    return drawn.at[tuple(place)].set(low).at[tuple(beside)].set(top_value)


def shard_levels(key, dims, split, low, largest):
    def one(dim, blocks):
        steps = jax.random.uniform(jax.random.fold_in(jax.random.fold_in(key, 6), dim), (blocks,), jnp.float32, low / len(split), largest / len(split))
        return jnp.repeat(jnp.exp(steps), dims[dim] // blocks).reshape((-1,) + (1,) * (len(dims) - dim - 1))

    gain = one(*split[0])
    for cut in split[1:]:
        gain = gain * one(*cut)
    return gain


def centred(own_key, shape, deviation, limit, shards=(), kind=jnp.bfloat16):
    drawn = jax.random.normal(own_key, shape, jnp.float32) * deviation
    if len(shards) > 0:
        drawn = shard_levels(own_key, shape, shards, -0.22, 0.18) * drawn
    return jnp.clip(drawn, min=-limit, max=limit).astype(kind)


def setup_inputs(seed: int = 0) -> dict:
    key_list = jax.random.split(jax.random.key(seed), 5)
    g_less = centred(key_list[0], (NE, NB, ORB, ORB), 1.0, 6.0, ((0, 8), (1, 32)))
    g_great = centred(key_list[1], (NE, NB, ORB, ORB), 1.0, 6.0, ((0, 8), (1, 32)))
    coupling = centred(key_list[2], (NB, 3, ORB, ORB), (3 * ORB) ** -0.5, 0.3125, ((0, 32),))
    coupling_mask = plant((jax.random.randint(key_list[3], (NB, 2), 0, 4) < 3).astype(jnp.int32), jax.random.fold_in(key_list[3], 1), 0, 1)
    return dict(g_less=g_less, g_great=g_great, coupling=coupling, coupling_mask=coupling_mask)


def lag_order(series):
    return jnp.concatenate([series[2 * NE - NE // 2:], series[:NE // 2]], axis=0)

def polarize(pair):
    lesser, greater = pair
    lesser = lesser.astype(jnp.float32).reshape(NE, ORB * ORB)
    greater = jnp.swapaxes(greater, 1, 2).astype(jnp.float32).reshape(NE, ORB * ORB)
    spectrum = jnp.fft.rfft(lesser, n=2 * NE, axis=0) * jnp.conj(jnp.fft.rfft(greater, n=2 * NE, axis=0))
    series = jnp.fft.irfft(spectrum, n=2 * NE, axis=0)
    return (lag_order(series) / math.sqrt(NE)).reshape(NE, ORB, ORB)

def reference(g_less, g_great, coupling, coupling_mask):
    less_blocks = jnp.moveaxis(g_less, 1, 0)
    great_blocks = jnp.moveaxis(g_great, 1, 0)
    pol = lax.map(polarize, (less_blocks, great_blocks))
    empty_rim = jnp.zeros((1, NE, ORB, ORB), pol.dtype)
    padded = jnp.concatenate([empty_rim, pol, empty_rim], axis=0)
    present = coupling_mask.astype(jnp.float32)
    highest = lax.Precision.HIGHEST

    def screen(index):
        couple = coupling[index].astype(jnp.float32)
        factors = jnp.stack([present[index, 0], jnp.ones((), present.dtype), present[index, 1]])
        accumulated = jnp.zeros((NE, ORB, ORB), jnp.float32)
        for offset in range(3):
            neighbour = lax.dynamic_index_in_dim(padded, index + offset, 0, keepdims=False)
            halfway = jnp.einsum('ij,ejk->eik', couple[offset], neighbour, precision=highest)
            accumulated = accumulated + factors[offset] * jnp.einsum('eik,lk->eil', halfway, couple[offset], precision=highest)
        return accumulated.astype(jnp.bfloat16)
    screened = lax.map(screen, jnp.arange(NB, dtype=jnp.int32))

    def selfenergy(pair):
        lesser, interaction = pair
        lesser = lesser.astype(jnp.float32).reshape(NE, ORB * ORB)
        interaction = interaction.astype(jnp.float32).reshape(NE, ORB * ORB)
        circular = jnp.concatenate([interaction[NE // 2:], jnp.zeros((NE, ORB * ORB), interaction.dtype), interaction[:NE // 2]], axis=0)
        spectrum = jnp.fft.rfft(lesser, n=2 * NE, axis=0) * jnp.fft.rfft(circular, n=2 * NE, axis=0)
        convolved = jnp.fft.irfft(spectrum, n=2 * NE, axis=0)[:NE]
        return (convolved / math.sqrt(NE)).reshape(NE, ORB, ORB)
    sigma = lax.map(selfenergy, (less_blocks, screened))
    return jnp.moveaxis(sigma, 0, 1).astype(jnp.float32)
```

```python
import functools
import math

import jax
import jax.numpy as jnp
import numpy as np
from jax import lax
from jax.experimental import pallas as pl
from jax.experimental.pallas import tpu as pltpu
from jax.sharding import PartitionSpec as P

MESH = pl.DeviceIdType.MESH
F32, BF16 = jnp.float32, jnp.bfloat16

GROUPS = 8
ORB = 128
NE = 256
ROWS = ORB // GROUPS
SHARE = NE // GROUPS
HALF = SHARE // 2
PERIOD = NE + NE // 2
FREQ = PERIOD // 2
CHUNKS = 4
PER = ROWS // CHUNKS
PAIRS = ROWS // 2


def tables():
    freq = 2 * np.arange(FREQ) + 1
    result = []
    for points in (np.arange(NE), np.arange(NE) - NE // 2):
        angle = np.pi * ((freq[:, None] * points[None, :]) % (2 * PERIOD)) / PERIOD
        whole = np.concatenate([np.cos(angle), np.sin(angle)], axis=0).astype(np.float32)
        upper = whole.astype(jnp.bfloat16)
        lower = (whole - upper.astype(np.float32)).astype(jnp.bfloat16)
        result.append(np.stack([upper, lower]))
    return result


def swap_matrix():
    row = np.arange(ROWS * ROWS)
    return (row[None, :] == ((row % ROWS) * ROWS + row // ROWS)[:, None]).astype(jnp.bfloat16)


def offset_of(k):
    return (3 * k) % GROUPS


def peer(me, k, sign):
    step = offset_of(k)
    x = (me + sign * (step % 4) + 4) % 4
    y = (me // 4 + step // 4) % 2
    return y * 4 + x


def dot(a, b):
    return jnp.dot(a, b, preferred_element_type=F32)


def side_by_side(a, b):
    return jnp.concatenate([a, b], axis=1)


def kernel(
    less_hbm, great_hbm, coupling_ref, mask_ref, fwd_e_hbm, fwd_l_hbm, inv_l_hbm, inv_e_hbm, swap_hbm,
    out_hbm,
    less, great, fwd_e, fwd_l, inv_l, inv_e, swap,
    less_out, great_out, less_in, great_in, spec, pol, pol_out, pol_in, near, turned, half, scr, scr_out, scr_in, sig, sig_out, sig_in,
    load_sem, store_sem,
    less_s, less_r, great_s, great_r, pol_s, pol_r, near_s, near_r, scr_s, scr_r, sig_s, sig_r,
):
    me = lax.axis_index("energy")
    block = lax.axis_index("block")
    n_blocks = lax.axis_size("block")
    has_before, has_after = block > 0, block < n_blocks - 1

    loads = [
        pltpu.make_async_copy(src, dst, load_sem.at[k])
        for k, (src, dst) in enumerate(
            [(less_hbm.at[:, 0], less), (swap_hbm, swap), (great_hbm.at[:, 0], great), (fwd_e_hbm, fwd_e),
             (inv_l_hbm, inv_l), (fwd_l_hbm, fwd_l), (inv_e_hbm, inv_e)]
        )
    ]
    for load in loads:
        load.start()

    barrier = pltpu.get_barrier_semaphore()
    for k in range(1, GROUPS):
        pl.semaphore_signal(barrier, inc=1, device_id={"energy": peer(me, k, 1)}, device_id_type=MESH)

    @pl.when(has_before)
    def _():
        pl.semaphore_signal(barrier, inc=1, device_id={"block": block - 1}, device_id_type=MESH)

    @pl.when(has_after)
    def _():
        pl.semaphore_signal(barrier, inc=1, device_id={"block": block + 1}, device_id_type=MESH)

    def exchange(first, second):
        both = dot(swap[...], side_by_side(first, second)).astype(BF16)
        return both[:, :ORB].reshape(ROWS, ROWS, ORB), both[:, ORB:].reshape(ROWS, ROWS, ORB)

    def rows_of(k):
        return pl.ds(pl.multiple_of(peer(me, k, 1) * ROWS, ROWS), ROWS)

    def share_of(k):
        return pl.multiple_of(peer(me, k, 1) * SHARE, SHARE)

    my_rows = pl.ds(pl.multiple_of(me * ROWS, ROWS), ROWS)
    my_share = pl.multiple_of(me * SHARE, SHARE)

    def by_rows(source, k):
        rows = rows_of(k)
        return exchange(
            source[0:HALF, rows, :].reshape(ROWS * ROWS, ORB),
            source[HALF:SHARE, rows, :].reshape(ROWS * ROWS, ORB),
        )

    loads[0].wait()
    loads[1].wait()
    low, high = by_rows(less, 0)
    less_in[:, pl.ds(my_share, HALF), :] = low
    less_in[:, pl.ds(my_share + HALF, HALF), :] = high

    def less_step(k, carry):
        low, high = by_rows(less, k)
        less_out[k, :, 0:HALF, :] = low
        less_out[k, :, HALF:SHARE, :] = high
        return carry

    lax.fori_loop(1, GROUPS, less_step, 0)

    pl.semaphore_wait(barrier, GROUPS - 1 + has_before.astype(jnp.int32) + has_after.astype(jnp.int32))

    def less_copy(k):
        return pltpu.make_async_remote_copy(
            src_ref=less_out.at[k], dst_ref=less_in.at[:, pl.ds(my_share, SHARE), :],
            send_sem=less_s.at[k], recv_sem=less_r.at[k],
            device_id={"energy": peer(me, k, 1)}, device_id_type=MESH,
        )

    for k in range(1, GROUPS):
        less_copy(k).start()

    loads[2].wait()

    def turn_step(m, carry):
        turned[m] = great[m].T
        return carry

    lax.fori_loop(0, SHARE, turn_step, 0, unroll=2)
    low, high = by_rows(turned, 0)
    great_in[:, pl.ds(my_share, HALF), :] = low
    great_in[:, pl.ds(my_share + HALF, HALF), :] = high

    def great_step(k, carry):
        low, high = by_rows(turned, k)
        great_out[k, :, 0:HALF, :] = low
        great_out[k, :, HALF:SHARE, :] = high
        return carry

    lax.fori_loop(1, GROUPS, great_step, 0)

    def great_copy(c, k):
        rows = pl.ds(c * PER, PER)
        return pltpu.make_async_remote_copy(
            src_ref=great_out.at[k, rows], dst_ref=great_in.at[rows, pl.ds(my_share, SHARE), :],
            send_sem=great_s.at[c, k], recv_sem=great_r.at[c, k],
            device_id={"energy": peer(me, k, 1)}, device_id_type=MESH,
        )

    for c in range(CHUNKS):
        for k in range(1, GROUPS):
            great_copy(c, k).start()

    for load in loads[3:]:
        load.wait()

    for k in range(1, GROUPS):
        less_copy(k).wait_recv()

    def forward(table, source, p):
        pair = side_by_side(source[2 * p], source[2 * p + 1])
        return dot(table[0], pair) + dot(table[1], pair)

    def less_transform(p, carry):
        spec[p] = forward(fwd_e, less_in, p)
        return carry

    lax.fori_loop(0, PAIRS, less_transform, 0)

    scale = 1.0 / (FREQ * math.sqrt(NE))

    def backward(table, real, imag, p, result):
        both = jnp.concatenate([real.astype(BF16), imag.astype(BF16)], axis=0)
        value = ((dot(table[0], both) + dot(table[1], both)) * scale).astype(BF16)
        result[2 * p] = value[:, :ORB]
        result[2 * p + 1] = value[:, ORB:]

    def pol_step(p, carry):
        great_spec = forward(fwd_e, great_in, p)
        a_cos, a_sin = spec[p, :FREQ, :], spec[p, FREQ:, :]
        b_cos, b_sin = great_spec[:FREQ], great_spec[FREQ:]
        backward(inv_l, a_cos * b_cos + a_sin * b_sin, a_sin * b_cos - a_cos * b_sin, p, pol)
        return carry

    for c in range(CHUNKS):
        for k in range(1, GROUPS):
            great_copy(c, k).wait_recv()
        lax.fori_loop(c * PAIRS // CHUNKS, (c + 1) * PAIRS // CHUNKS, pol_step, 0)

    def to_share(source, k):
        first = share_of(k)
        return exchange(
            source[:, pl.ds(first, HALF), :].reshape(ROWS * ROWS, ORB),
            source[:, pl.ds(first + HALF, HALF), :].reshape(ROWS * ROWS, ORB),
        )

    low, high = to_share(pol, 0)
    pol_in[0, :, my_rows, :] = low
    pol_in[1, :, my_rows, :] = high

    def pol_out_step(k, carry):
        low, high = to_share(pol, k)
        pol_out[0, k] = low
        pol_out[1, k] = high
        return carry

    lax.fori_loop(1, GROUPS, pol_out_step, 0)

    def pol_copy(h, k):
        return pltpu.make_async_remote_copy(
            src_ref=pol_out.at[h, k], dst_ref=pol_in.at[h, :, my_rows, :],
            send_sem=pol_s.at[h, k], recv_sem=pol_r.at[h, k],
            device_id={"energy": peer(me, k, 1)}, device_id_type=MESH,
        )

    for h in range(2):
        for k in range(1, GROUPS):
            pol_copy(h, k).start()

    def near_copy(h, side, k):
        rows = pl.ds(pl.multiple_of(peer(me, k, -1) * ROWS, ROWS), ROWS)
        return pltpu.make_async_remote_copy(
            src_ref=pol_in.at[h, :, rows, :], dst_ref=near.at[h, side, :, rows, :],
            send_sem=near_s.at[h, side, k], recv_sem=near_r.at[h, side, k],
            device_id={"block": block + 1 - 2 * side}, device_id_type=MESH,
        )

    @pl.when(jnp.logical_not(has_before))
    def _():
        near[:, 0] = jnp.zeros((2, HALF, ORB, ORB), BF16)

    @pl.when(jnp.logical_not(has_after))
    def _():
        near[:, 1] = jnp.zeros((2, HALF, ORB, ORB), BF16)

    def scaled(t, factor):
        return (coupling_ref[0, t].astype(F32) * factor).astype(BF16)

    weights = [
        scaled(0, mask_ref[0, 0].astype(F32)), coupling_ref[0, 1], scaled(2, mask_ref[0, 1].astype(F32)),
    ]

    def halfway(h, t):
        def step(p, carry):
            if t == 1:
                pair = side_by_side(pol_in[h, 2 * p], pol_in[h, 2 * p + 1])
            else:
                pair = side_by_side(near[h, t // 2, 2 * p], near[h, t // 2, 2 * p + 1])
            value = dot(weights[t], pair).astype(BF16)
            half[t, 2 * p] = value[:, :ORB]
            half[t, 2 * p + 1] = value[:, ORB:]
            return carry

        lax.fori_loop(0, HALF // 2, step, 0)

    across = jnp.concatenate([coupling_ref[0, t].T for t in range(3)], axis=0)

    def scr_copy(h, k):
        return pltpu.make_async_remote_copy(
            src_ref=scr_out.at[h, k], dst_ref=scr_in.at[:, pl.ds(my_share + h * HALF, HALF), :],
            send_sem=scr_s.at[h, k], recv_sem=scr_r.at[h, k],
            device_id={"energy": peer(me, k, 1)}, device_id_type=MESH,
        )

    for h in range(2):
        for k in range(GROUPS):
            if k > 0:
                pol_copy(h, k).wait_recv()

            @pl.when(has_after)
            def _():
                near_copy(h, 0, k).start()

            @pl.when(has_before)
            def _():
                near_copy(h, 1, k).start()

        halfway(h, 1)

        @pl.when(has_before)
        def _():
            for k in range(GROUPS):
                near_copy(h, 0, k).wait_recv()

        halfway(h, 0)

        @pl.when(has_after)
        def _():
            for k in range(GROUPS):
                near_copy(h, 1, k).wait_recv()

        halfway(h, 2)

        def scr_step(p, carry):
            both = jnp.concatenate(
                [half[t, pl.ds(2 * p, 2)].reshape(2 * ORB, ORB) for t in range(3)], axis=1
            )
            scr[pl.ds(2 * p, 2)] = dot(both, across).astype(BF16).reshape(2, ORB, ORB)
            return carry

        lax.fori_loop(0, HALF // 2, scr_step, 0)

        def scr_part(k):
            return scr[:, rows_of(k), :].reshape(ROWS * ROWS, ORB)

        def scr_out_step(p, carry):
            first, second = exchange(scr_part(2 * p), scr_part(2 * p + 1))
            scr_out[h, 2 * p] = first
            scr_out[h, 2 * p + 1] = second
            return carry

        lax.fori_loop(0, GROUPS // 2, scr_out_step, 0)
        scr_in[:, pl.ds(my_share + h * HALF, HALF), :] = scr_out[h, 0]
        for k in range(1, GROUPS):
            scr_copy(h, k).start()

    for h in range(2):
        for k in range(1, GROUPS):
            scr_copy(h, k).wait_recv()

    def sig_step(p, carry):
        scr_spec = forward(fwd_l, scr_in, p)
        a_cos, a_sin = spec[p, :FREQ, :], spec[p, FREQ:, :]
        b_cos, b_sin = scr_spec[:FREQ], scr_spec[FREQ:]
        backward(inv_e, a_cos * b_cos - a_sin * b_sin, a_cos * b_sin + a_sin * b_cos, p, sig)
        return carry

    lax.fori_loop(0, PAIRS, sig_step, 0)

    low, high = to_share(sig, 0)
    sig_in[0:HALF, my_rows, :] = low
    sig_in[HALF:SHARE, my_rows, :] = high

    def sig_copy(k):
        return pltpu.make_async_remote_copy(
            src_ref=sig_out.at[k], dst_ref=sig_in.at[:, my_rows, :],
            send_sem=sig_s.at[k], recv_sem=sig_r.at[k],
            device_id={"energy": peer(me, k, 1)}, device_id_type=MESH,
        )

    def sig_out_step(k, carry):
        low, high = to_share(sig, k)
        sig_out[k, 0:HALF] = low
        sig_out[k, HALF:SHARE] = high
        return carry

    lax.fori_loop(1, GROUPS, sig_out_step, 0)
    for k in range(1, GROUPS):
        sig_copy(k).start()

    for k in range(1, GROUPS):
        less_copy(k).wait_send()
        for c in range(CHUNKS):
            great_copy(c, k).wait_send()
        for h in range(2):
            pol_copy(h, k).wait_send()
            scr_copy(h, k).wait_send()

    for h in range(2):
        for k in range(GROUPS):

            @pl.when(has_after)
            def _():
                near_copy(h, 0, k).wait_send()

            @pl.when(has_before)
            def _():
                near_copy(h, 1, k).wait_send()

    for k in range(1, GROUPS):
        sig_copy(k).wait_recv()
    store = pltpu.make_async_copy(sig_in, out_hbm, store_sem)
    store.start()
    for k in range(1, GROUPS):
        sig_copy(k).wait_send()
    store.wait()


def shards(g_less, g_great, coupling, coupling_mask):
    energy, lag = tables()
    any_space = pl.BlockSpec(memory_space=pl.ANY)
    vmem = pl.BlockSpec(memory_space=pltpu.VMEM)
    share = (SHARE, ORB, ORB)
    group = (ROWS, NE, ORB)
    to_rows = (GROUPS, ROWS, SHARE, ORB)
    dma = pltpu.SemaphoreType.DMA
    sigma = pl.pallas_call(
        kernel,
        out_shape=jax.ShapeDtypeStruct(share, BF16),
        in_specs=[any_space, any_space, vmem, pl.BlockSpec(memory_space=pltpu.SMEM)] + [any_space] * 5,
        out_specs=any_space,
        scratch_shapes=[
            pltpu.VMEM(share, BF16),
            pltpu.VMEM(share, BF16),
            pltpu.VMEM((2, PERIOD, NE), BF16),
            pltpu.VMEM((2, PERIOD, NE), BF16),
            pltpu.VMEM((2, NE, PERIOD), BF16),
            pltpu.VMEM((2, NE, PERIOD), BF16),
            pltpu.VMEM((NE, NE), BF16),
            pltpu.VMEM(to_rows, BF16),
            pltpu.VMEM(to_rows, BF16),
            pltpu.VMEM(group, BF16),
            pltpu.VMEM(group, BF16),
            pltpu.VMEM((PAIRS, PERIOD, 2 * ORB), F32),
            pltpu.VMEM(group, BF16),
            pltpu.VMEM((2, GROUPS, HALF, ROWS, ORB), BF16),
            pltpu.VMEM((2, HALF, ORB, ORB), BF16),
            pltpu.VMEM((2, 2, HALF, ORB, ORB), BF16),
            pltpu.VMEM(share, BF16),
            pltpu.VMEM((3, HALF, ORB, ORB), BF16),
            pltpu.VMEM((HALF, ORB, ORB), BF16),
            pltpu.VMEM((2, GROUPS, ROWS, HALF, ORB), BF16),
            pltpu.VMEM(group, BF16),
            pltpu.VMEM(group, BF16),
            pltpu.VMEM((GROUPS, SHARE, ROWS, ORB), BF16),
            pltpu.VMEM(share, BF16),
            dma((7,)),
            dma,
            dma((GROUPS,)), dma((GROUPS,)),
            dma((CHUNKS, GROUPS)), dma((CHUNKS, GROUPS)),
            dma((2, GROUPS)), dma((2, GROUPS)),
            dma((2, 2, GROUPS)), dma((2, 2, GROUPS)),
            dma((2, GROUPS)), dma((2, GROUPS)),
            dma((GROUPS,)), dma((GROUPS,)),
        ],
        compiler_params=pltpu.CompilerParams(
            collective_id=0, has_side_effects=True, vmem_limit_bytes=56 * 1024 * 1024
        ),
        name="gw",
    )(
        g_less, g_great, coupling, coupling_mask,
        jnp.asarray(energy), jnp.asarray(lag),
        jnp.asarray(np.ascontiguousarray(lag.transpose(0, 2, 1))),
        jnp.asarray(np.ascontiguousarray(energy.transpose(0, 2, 1))),
        jnp.asarray(swap_matrix()),
    )
    return sigma.astype(F32)[:, None]


def solution(mesh):
    return jax.shard_map(
        shards,
        mesh=mesh,
        in_specs=(
            P("energy", "block", None, None),
            P("energy", "block", None, None),
            P("block", None, None, None),
            P("block", None),
        ),
        out_specs=P("energy", "block", None, None),
        check_vma=False,
    )
```
